32 devices in a mesh: gx: 8 (over z, x), gy: 4 (over y, core).
Axes of the slice: x: 2, y: 2, z: 4, core: 2. Of those that a mesh axis runs over, the one named last changes fastest.
Arguments:
- design: float32 [128, 256, 512], P('gx', 'gy'), may hold values from 0 to 1, as said below
- sensitivity: float32 [128, 256, 512], P('gx', 'gy'), may hold values from 0.1 to 10
- solid_mask: int32 [128, 256, 512], P('gx', 'gy'), may hold values 0 or 1
Outputs:
- new_design: float32 [128, 256, 512], P('gx', 'gy')
- objective_grad: float32 [128, 256, 512], P('gx', 'gy')
- multiplier: float32 [], replicated
The draws below stay inside these ranges and needn't reach their ends.
Inputs may be any that keep to these rules, and one draw needn't show every extreme that they name: design densities lie strictly between 0 and 1.
All inputs are finite; a program needn't handle non-finite values. No bound on the sum of `solid_mask` on one device may be relied on, other than what follows from the above.
Results may differ from the reference program's by a relative error of at most 0.0003.
Values sent between devices are 32-bit elements; how exact they have to be, the bound alone decides.
A program may use at most 64 MiB of HBM per device.

```python
import math
import jax
import jax.numpy as jnp
from jax import lax

NZ = 512
RADIUS = 8
DUAL_ITERS = 2
NX = 128
NY = 256


def box_sum(field_in, which_axis):
    return jnp.roll(field_in, 1, which_axis) + field_in + jnp.roll(field_in, -1, which_axis)


def draw_design(key, part):
    across_x = (jnp.arange(NX, dtype=jnp.float32) + 0.5) / NX
    across_y = (jnp.arange(NY, dtype=jnp.float32) + 0.5) / NY
    trend_part = 0.3 * (across_x[:, None, None] + across_y[None, :, None] - 1.0)
    white_noise = jax.random.normal(key, (NX, NY, NZ), jnp.float32)
    amplitude = 0.35
    smooth_part = white_noise
    for which_axis in range(3):
        smooth_part = box_sum(box_sum(smooth_part, which_axis), which_axis)
    smooth_part = smooth_part * 0.012075
    return jnp.clip(0.5 + trend_part + amplitude * smooth_part, 0.01, 0.99)


def with_ends(result, stream_key, smallest, largest):
    shape = result.shape
    index_at = [jax.random.randint(jax.random.fold_in(stream_key, axis), (), 0, shape[axis]) for axis in range(len(shape))]
    result = result.at[tuple(index_at)].set(smallest)
    longest = shape.index(max(shape))
    index_at[longest] = (index_at[longest] + 1) % shape[longest]
    return result.at[tuple(index_at)].set(largest)


def shard_levels(key, shape, split, low, high):
    loudness, own = 1.0, jax.random.fold_in(key, 6)
    for position, shards_of in split:
        steps = jnp.exp(jax.random.uniform(jax.random.fold_in(own, position), (shards_of,), jnp.float32, low / len(split), high / len(split)))
        loudness = loudness * jnp.repeat(steps, shape[position] // shards_of).reshape([-1 if axis == position else 1 for axis in range(len(shape))])
    return loudness


def setup_inputs(seed: int = 0) -> dict:
    splits = jax.random.split(jax.random.key(seed), 4)
    design = draw_design(jax.random.fold_in(splits[3], 71), 0)
    sensitivity = jnp.clip(jnp.exp(math.log(10.0) - 4.6051702 * jax.random.uniform(splits[1], (NX, NY, NZ), jnp.float32) ** shard_levels(splits[1], (NX, NY, NZ), ((0, 8), (1, 4)), -0.2, 0.2)), 0.1, 10.0)
    solid_mask = with_ends((jax.random.randint(splits[2], (NX, NY, NZ), 0, 8) < 1).astype(jnp.int32), jax.random.fold_in(splits[2], 1), 0, 1)
    return {"design": design, "sensitivity": sensitivity, "solid_mask": solid_mask}


beta_value = 4.0
eta_value = 0.5
volume_share = 0.4
move_limit = 0.2
asym_gap = 0.5

def band(count):
    index = jnp.arange(count)
    gap = jnp.abs(index[:, None] - index[None, :])
    return jnp.maximum(RADIUS + 1 - gap, 0).astype(jnp.float32)

def smooth(field, band_x, band_y, band_z):
    high = lax.Precision.HIGHEST
    out = jnp.einsum('abc,ck->abk', field, band_z, precision=high)
    out = jnp.einsum('ia,abk->ibk', band_x, out, precision=high)
    out = jnp.einsum('jb,ibk->ijk', band_y, out, precision=high)
    return out

def dual_point(lam, design, p_zero, q_zero, p_one, q_one, lower, upper):
    low = design - asym_gap
    upp = design + asym_gap
    a_root = jnp.sqrt(p_zero + lam * p_one)
    b_root = jnp.sqrt(q_zero + lam * q_one)
    raw = (a_root * low + b_root * upp) / (a_root + b_root)
    inside = jnp.logical_and(raw > lower, raw < upper).astype(jnp.float32)
    point = jnp.clip(raw, lower, upper)
    value = p_one / (upp - point) + q_one / (point - low)
    moved = (upp - low) * (a_root * q_one / (2.0 * b_root) - b_root * p_one / (2.0 * a_root)) / (a_root + b_root) ** 2
    change = (p_one / (upp - point) ** 2 - q_one / (point - low) ** 2) * inside * moved
    return (point, value, change)

def reference(design, sensitivity, solid_mask):
    band_x = band(NX)
    band_y = band(NY)
    band_z = band(NZ)
    weight_sum = lax.optimization_barrier(jnp.sum(band_x, 1))[:, None, None] * lax.optimization_barrier(jnp.sum(band_y, 1))[None, :, None] * lax.optimization_barrier(jnp.sum(band_z, 1))[None, None, :]
    filtered = smooth(design, band_x, band_y, band_z) / weight_sum
    shifted = jnp.tanh(beta_value * (filtered - eta_value))
    scale = jnp.tanh(beta_value * eta_value) + jnp.tanh(beta_value * (1.0 - eta_value))
    free = (1 - solid_mask).astype(jnp.float32)
    physical = jnp.where(solid_mask == 1, 1.0, (jnp.tanh(beta_value * eta_value) + shifted) / scale)
    slope = beta_value * (1.0 - shifted * shifted) / scale * free
    objective_grad = smooth(-sensitivity * slope / weight_sum, band_x, band_y, band_z)
    volume_grad = smooth(slope / weight_sum, band_x, band_y, band_z)
    p_zero = 0.25 * (1.001 * jnp.maximum(objective_grad, 0.0) + 0.001 * jnp.maximum(-objective_grad, 0.0) + 1e-05)
    q_zero = 0.25 * (0.001 * jnp.maximum(objective_grad, 0.0) + 1.001 * jnp.maximum(-objective_grad, 0.0) + 1e-05)
    p_one = 0.25 * 1.001 * volume_grad * free
    q_one = 0.25 * 0.001 * volume_grad * free
    lower = jnp.maximum(0.0, design - move_limit)
    upper = jnp.minimum(1.0, design + move_limit)
    offset = jnp.mean(physical) - volume_share - jnp.mean((p_one + q_one) / asym_gap)
    lam = jnp.float32(1.0)
    for turn in range(DUAL_ITERS):
        point, value, change = dual_point(lam, design, p_zero, q_zero, p_one, q_one, lower, upper)
        level = jnp.mean(value) + offset
        rate = jnp.mean(change)
        lam = lam * jnp.exp(-level / (lam * rate - 1e-06))
    point, value, change = dual_point(lam, design, p_zero, q_zero, p_one, q_one, lower, upper)
    new_design = jnp.where(solid_mask == 1, design, point)
    return (new_design, objective_grad, lam)
```

```python
import functools
import math

import jax
import jax.numpy as jnp
from jax import lax
from jax.experimental import pallas as pl
from jax.experimental.pallas import tpu as pltpu
from jax.sharding import PartitionSpec as P

RADIUS = 8
DUAL_ITERS = 2
SPAN = RADIUS + 1
MESH = pl.DeviceIdType.MESH

beta_value = 4.0
eta_value = 0.5
volume_share = 0.4
move_limit = 0.2
asym_gap = 0.5
TANH_MID = math.tanh(beta_value * eta_value)
SCALE = math.tanh(beta_value * eta_value) + math.tanh(beta_value * (1.0 - eta_value))


def missing(distance):
    out = jnp.maximum(RADIUS - distance, 0)
    return (out * (out + 1)) // 2


def cover(cell, total):
    return (SPAN * SPAN - missing(cell) - missing(total - 1 - cell)).astype(jnp.float32)


def split2(x):
    hi = x.astype(jnp.bfloat16)
    lo = (x - hi.astype(jnp.float32)).astype(jnp.bfloat16)
    return hi, lo


def filter_zy(src, dst, group):
    rows, wide, depth = src.shape
    ry = wide - 2 * RADIUS
    jj = lax.broadcasted_iota(jnp.int32, (ry, wide), 0)
    bb = lax.broadcasted_iota(jnp.int32, (ry, wide), 1)
    band_y = jnp.maximum(SPAN - jnp.abs(jj + RADIUS - bb), 0).astype(jnp.float32).astype(jnp.bfloat16)
    cc = lax.broadcasted_iota(jnp.int32, (depth, depth), 0)
    kk = lax.broadcasted_iota(jnp.int32, (depth, depth), 1)
    band_z = jnp.maximum(SPAN - jnp.abs(cc - kk), 0).astype(jnp.float32).astype(jnp.bfloat16)

    def body(g, carry):
        his, los = [], []
        for r in range(group):
            hi, lo = split2(src[g * group + r])
            out = jnp.dot(band_y, hi, preferred_element_type=jnp.float32) + jnp.dot(
                band_y, lo, preferred_element_type=jnp.float32
            )
            hi, lo = split2(out)
            his.append(hi)
            los.append(lo)
        both = jnp.dot(
            jnp.concatenate(his + los, 0), band_z, preferred_element_type=jnp.float32
        )
        half = group * ry
        total = both[:half] + both[half:]
        for r in range(group):
            dst[g * group + r] = total[r * ry : (r + 1) * ry]
        return carry

    lax.fori_loop(0, rows // group, body, 0)


def filter_x(src, tile, emit):
    count = src.shape[0] - 2 * RADIUS
    load = lambda i: src[i, tile, :]
    box = load(0)
    for k in range(1, SPAN):
        box = box + load(k)
    window = [box]
    for n in range(1, SPAN):
        box = box + (load(n + RADIUS) - load(n - 1))
        window.append(box)
    total = window[0]
    for k in range(1, SPAN):
        total = total + window[k]
    emit(0, total)
    for i in range(1, count):
        n = i + RADIUS
        box = box + (load(n + RADIUS) - load(n - 1))
        total = total + (box - window[i - 1])
        window.append(box)
        emit(i, total)


(DES_UP, DES_DN, MASK, SENS, AFLD, A_UP, A_DN, V_UP, V_DN, O_UP, O_DN, VB, OB,
 VY_UP, VY_DN, OY_UP, OY_DN, COUNT) = range(18)


def kernel(design, sens, mask, obj_out, vol_out, phys_out, dbuf, afull, abuf, mbuf, sbuf, vbuf, obuf,
           vx, ox, vback, oback, send_sems, recv_sems, local_sems):
    rows, ry, depth = design.shape
    half = depth // 2
    gx, gy = lax.axis_index("gx"), lax.axis_index("gy")
    nx, ny = lax.axis_size("gx"), lax.axis_size("gy")
    par = lax.rem(gx, 2)
    pair = gx // 2
    partner = gx + 1 - 2 * par
    has_xl, has_xr = gx >= 2, gx < nx - 2
    has_yl, has_yr = gy >= 1, gy < ny - 1
    xl, xr, yl, yr = (gx - 2, gy), (gx + 2, gy), (gx, gy - 1), (gx, gy + 1)
    mate = (partner, gy)

    barrier = pltpu.get_barrier_semaphore()

    def greet(dev):
        pl.semaphore_signal(barrier, inc=1, device_id=dev, device_id_type=MESH)

    greet(mate)
    for cond, dev in ((has_xl, xl), (has_xr, xr), (has_yl, yl), (has_yr, yr)):
        pl.when(cond)(functools.partial(greet, dev))

    own = pl.ds(pl.multiple_of(par * half, 128), half)
    other = pl.ds(pl.multiple_of((1 - par) * half, 128), half)
    my_rows = pl.ds(par * rows, rows)
    mate_rows = pl.ds((1 - par) * rows, rows)
    mid = pl.ds(RADIUS, ry)

    l_des = pltpu.make_async_copy(design, dbuf.at[:, mid, :], local_sems.at[0])
    l_mask = pltpu.make_async_copy(mask.at[:, :, own], mbuf.at[my_rows], local_sems.at[1])
    l_sens = pltpu.make_async_copy(sens.at[:, :, own], sbuf.at[my_rows], local_sems.at[2])
    l_des.start()
    l_mask.start()
    l_sens.start()

    count = 1 + sum(c.astype(jnp.int32) for c in (has_xl, has_xr, has_yl, has_yr))
    pl.semaphore_wait(barrier, count)

    def remote(idx, src, dst, dev):
        return pltpu.make_async_remote_copy(
            src_ref=src, dst_ref=dst, send_sem=send_sems.at[idx], recv_sem=recv_sems.at[idx],
            device_id=dev, device_id_type=MESH,
        )

    def y_pair(up, dn, src, off, buf):
        return (
            remote(up, src.at[:, pl.ds(off + ry - RADIUS, RADIUS), :], buf.at[:, pl.ds(0, RADIUS), :], yr),
            remote(dn, src.at[:, pl.ds(off, RADIUS), :], buf.at[:, pl.ds(RADIUS + ry, RADIUS), :], yl),
        )

    def x_pair(up, dn, buf):
        return (
            remote(up, buf.at[pl.ds(2 * rows, RADIUS)], buf.at[pl.ds(0, RADIUS)], xr),
            remote(dn, buf.at[pl.ds(RADIUS, RADIUS)], buf.at[pl.ds(RADIUS + 2 * rows, RADIUS)], xl),
        )

    def begin(two, low, high):
        pl.when(high)(lambda: two[0].start())
        pl.when(low)(lambda: two[1].start())

    def finish(two, low, high):
        pl.when(low)(lambda: two[0].wait_recv())
        pl.when(high)(lambda: two[1].wait_recv())

    def sent(two, low, high):
        pl.when(high)(lambda: two[0].wait_send())
        pl.when(low)(lambda: two[1].wait_send())

    r_des = y_pair(DES_UP, DES_DN, design, 0, dbuf)
    begin(r_des, has_yl, has_yr)
    r_mask = remote(MASK, mask.at[:, :, other], mbuf.at[my_rows], mate)
    r_mask.start()

    def zero_y(buf):
        zero = jnp.zeros((rows, RADIUS, depth), jnp.float32)

        @pl.when(jnp.logical_not(has_yl))
        def _():
            buf[:, 0:RADIUS, :] = zero

        @pl.when(jnp.logical_not(has_yr))
        def _():
            buf[:, RADIUS + ry :, :] = zero

    def zero_x(buf):
        zero = jnp.zeros((RADIUS, ry, half), jnp.float32)

        @pl.when(jnp.logical_not(has_xl))
        def _():
            buf[0:RADIUS] = zero

        @pl.when(jnp.logical_not(has_xr))
        def _():
            buf[RADIUS + 2 * rows :] = zero

    for buf in (dbuf, vback, oback):
        zero_y(buf)
    for buf in (abuf, vbuf, obuf):
        zero_x(buf)

    group = 4 if rows % 4 == 0 else 1
    l_des.wait()
    finish(r_des, has_yl, has_yr)
    filter_zy(dbuf, afull, group)
    r_a = remote(AFLD, afull.at[:, :, other], abuf.at[pl.ds(RADIUS + par * rows, rows)], mate)
    r_a.start()
    r_sens = remote(SENS, sens.at[:, :, other], sbuf.at[my_rows], mate)
    r_sens.start()
    l_a = pltpu.make_async_copy(afull.at[:, :, own], abuf.at[pl.ds(RADIUS + par * rows, rows)], local_sems.at[3])
    l_a.start()
    l_a.wait()
    r_a.wait_recv()
    x_a = x_pair(A_UP, A_DN, abuf)
    begin(x_a, has_xl, has_xr)
    l_mask.wait()
    r_mask.wait_recv()
    finish(x_a, has_xl, has_xr)

    total_x, total_y = rows * nx, ry * ny
    wz = cover(par * half + lax.broadcasted_iota(jnp.int32, (8, half), 1), depth)

    phys_out[...] = jnp.zeros_like(phys_out)

    def stage_one(j, carry):
        tile = pl.ds(pl.multiple_of(j * 8, 8), 8)
        wy = cover(gy * ry + j * 8 + lax.broadcasted_iota(jnp.int32, (8, half), 0), total_y)
        wyz = wy * wz

        def emit(i, value):
            weight = wyz * cover(pair * (2 * rows) + i, total_x)
            inv = 1.0 / weight
            shifted = jnp.tanh(beta_value * (value * inv - eta_value))
            solid = mbuf[i, tile, :]
            free = (1 - solid).astype(jnp.float32)
            phys_out[...] += jnp.where(solid == 1, 1.0, (TANH_MID + shifted) * (1.0 / SCALE))
            vbuf[RADIUS + i, tile, :] = (beta_value / SCALE) * (1.0 - shifted * shifted) * free * inv

        filter_x(abuf, tile, emit)
        return carry

    lax.fori_loop(0, ry // 8, stage_one, 0)
    x_v = x_pair(V_UP, V_DN, vbuf)
    begin(x_v, has_xl, has_xr)
    finish(x_v, has_xl, has_xr)

    def x_only(src, dst):
        def body(j, carry):
            tile = pl.ds(pl.multiple_of(j * 8, 8), 8)

            def emit(i, value):
                dst[i, tile, :] = value

            filter_x(src, tile, emit)
            return carry

        lax.fori_loop(0, ry // 8, body, 0)

    x_only(vbuf, vx)
    r_vb = remote(VB, vx.at[mate_rows], vback.at[:, mid, own], mate)
    r_vb.start()
    l_vb = pltpu.make_async_copy(vx.at[my_rows], vback.at[:, mid, own], local_sems.at[4])
    l_vb.start()

    l_sens.wait()
    r_sens.wait_recv()

    def times(i, carry):
        obuf[RADIUS + i] = -sbuf[i] * vbuf[RADIUS + i]
        return carry

    lax.fori_loop(0, 2 * rows, times, 0)
    x_o = x_pair(O_UP, O_DN, obuf)
    begin(x_o, has_xl, has_xr)
    finish(x_o, has_xl, has_xr)
    x_only(obuf, ox)
    r_ob = remote(OB, ox.at[mate_rows], oback.at[:, mid, own], mate)
    r_ob.start()
    l_ob = pltpu.make_async_copy(ox.at[my_rows], oback.at[:, mid, own], local_sems.at[5])
    l_ob.start()

    l_vb.wait()
    r_vb.wait_recv()
    y_v = y_pair(VY_UP, VY_DN, vback, RADIUS, vback)
    begin(y_v, has_yl, has_yr)
    finish(y_v, has_yl, has_yr)
    filter_zy(vback, vol_out, group)

    l_ob.wait()
    r_ob.wait_recv()
    y_o = y_pair(OY_UP, OY_DN, oback, RADIUS, oback)
    begin(y_o, has_yl, has_yr)
    finish(y_o, has_yl, has_yr)
    filter_zy(oback, obj_out, group)

    for one in (r_mask, r_a, r_sens, r_vb, r_ob):
        one.wait_send()
    for two in (r_des, y_v, y_o):
        sent(two, has_yl, has_yr)
    for two in (x_a, x_v, x_o):
        sent(two, has_xl, has_xr)


def gradients(design, sensitivity, solid_mask):
    rows, ry, depth = design.shape
    half = depth // 2
    f32 = jnp.float32
    wide = (rows, ry + 2 * RADIUS, depth)
    tall = (2 * rows + 2 * RADIUS, ry, half)
    strip = (2 * rows, ry, half)
    vmem = pl.BlockSpec(memory_space=pltpu.VMEM)
    return pl.pallas_call(
        kernel,
        out_shape=(
            jax.ShapeDtypeStruct((rows, ry, depth), f32),
            jax.ShapeDtypeStruct((rows, ry, depth), f32),
            jax.ShapeDtypeStruct((8, half), f32),
        ),
        in_specs=[pl.BlockSpec(memory_space=pl.ANY)] * 3,
        out_specs=(vmem, vmem, vmem),
        scratch_shapes=[
            pltpu.VMEM(wide, f32),
            pltpu.VMEM((rows, ry, depth), f32),
            pltpu.VMEM(tall, f32),
            pltpu.VMEM(strip, jnp.int32),
            pltpu.VMEM(strip, f32),
            pltpu.VMEM(tall, f32),
            pltpu.VMEM(tall, f32),
            pltpu.VMEM(strip, f32),
            pltpu.VMEM(strip, f32),
            pltpu.VMEM(wide, f32),
            pltpu.VMEM(wide, f32),
            pltpu.SemaphoreType.DMA((COUNT,)),
            pltpu.SemaphoreType.DMA((COUNT,)),
            pltpu.SemaphoreType.DMA((6,)),
        ],
        compiler_params=pltpu.CompilerParams(
            collective_id=0, has_side_effects=True, vmem_limit_bytes=56 * 1024 * 1024
        ),
    )(design, sensitivity, solid_mask)


def dual_point(lam, design, p_zero, q_zero, p_one, q_one, lower, upper):
    low = design - asym_gap
    upp = design + asym_gap
    a_root = jnp.sqrt(p_zero + lam * p_one)
    b_root = jnp.sqrt(q_zero + lam * q_one)
    raw = (a_root * low + b_root * upp) / (a_root + b_root)
    inside = jnp.logical_and(raw > lower, raw < upper).astype(jnp.float32)
    point = jnp.clip(raw, lower, upper)
    value = p_one / (upp - point) + q_one / (point - low)
    moved = (
        (upp - low)
        * (a_root * q_one / (2.0 * b_root) - b_root * p_one / (2.0 * a_root))
        / (a_root + b_root) ** 2
    )
    change = (p_one / (upp - point) ** 2 - q_one / (point - low) ** 2) * inside * moved
    return (point, value, change)


def per_device(design, sensitivity, solid_mask):
    rows_x, rows_y, depth = design.shape
    cell_count = float(rows_x * rows_y * depth * lax.axis_size("gx") * lax.axis_size("gy"))
    objective_grad, volume_grad, phys = gradients(design, sensitivity, solid_mask)
    free = (1 - solid_mask).astype(jnp.float32)
    p_zero = 0.25 * (
        1.001 * jnp.maximum(objective_grad, 0.0) + 0.001 * jnp.maximum(-objective_grad, 0.0) + 1e-05
    )
    q_zero = 0.25 * (
        0.001 * jnp.maximum(objective_grad, 0.0) + 1.001 * jnp.maximum(-objective_grad, 0.0) + 1e-05
    )
    p_one = 0.25 * 1.001 * volume_grad * free
    q_one = 0.25 * 0.001 * volume_grad * free
    lower = jnp.maximum(0.0, design - move_limit)
    upper = jnp.minimum(1.0, design + move_limit)
    base_local = jnp.sum((p_one + q_one) / asym_gap)
    mass_local = jnp.sum(phys) - volume_share * rows_x * rows_y * depth
    lam = jnp.float32(1.0)
    base_total, mass_total = lax.psum((base_local, mass_local), ("gx", "gy"))
    offset = mass_total / cell_count - base_total / cell_count
    for turn in range(DUAL_ITERS):
        point, value, change = dual_point(lam, design, p_zero, q_zero, p_one, q_one, lower, upper)
        value_total, change_total = lax.psum((jnp.sum(value), jnp.sum(change)), ("gx", "gy"))
        level = value_total / cell_count + offset
        rate = change_total / cell_count
        lam = lam * jnp.exp(-level / (lam * rate - 1e-06))
    point, value, change = dual_point(lam, design, p_zero, q_zero, p_one, q_one, lower, upper)
    new_design = jnp.where(solid_mask == 1, design, point)
    return (new_design, objective_grad, lam)


def solution(mesh):
    return jax.shard_map(
        per_device,
        mesh=mesh,
        in_specs=(P("gx", "gy", None), P("gx", "gy", None), P("gx", "gy", None)),
        out_specs=(P("gx", "gy", None), P("gx", "gy", None), P()),
        check_vma=False,
    )
```

```python
import functools
import math

import jax
import jax.numpy as jnp
from jax import lax
from jax.experimental import pallas as pl
from jax.experimental.pallas import tpu as pltpu
from jax.sharding import PartitionSpec as P

RADIUS = 8
DUAL_ITERS = 2
SPAN = RADIUS + 1
MESH = pl.DeviceIdType.MESH

beta_value = 4.0
eta_value = 0.5
volume_share = 0.4
move_limit = 0.2
asym_gap = 0.5
TANH_MID = math.tanh(beta_value * eta_value)
SCALE = math.tanh(beta_value * eta_value) + math.tanh(beta_value * (1.0 - eta_value))


def missing(distance):
    out = jnp.maximum(RADIUS - distance, 0)
    return (out * (out + 1)) // 2


def cover(cell, total):
    return (SPAN * SPAN - missing(cell) - missing(total - 1 - cell)).astype(jnp.float32)


def split2(x):
    hi = x.astype(jnp.bfloat16)
    lo = (x - hi.astype(jnp.float32)).astype(jnp.bfloat16)
    return hi, lo


def filter_zy(src, dst, group):
    rows, wide, depth = src.shape
    ry = wide - 2 * RADIUS
    jj = lax.broadcasted_iota(jnp.int32, (ry, wide), 0)
    bb = lax.broadcasted_iota(jnp.int32, (ry, wide), 1)
    band_y = jnp.maximum(SPAN - jnp.abs(jj + RADIUS - bb), 0).astype(jnp.float32).astype(jnp.bfloat16)
    cc = lax.broadcasted_iota(jnp.int32, (depth, depth), 0)
    kk = lax.broadcasted_iota(jnp.int32, (depth, depth), 1)
    band_z = jnp.maximum(SPAN - jnp.abs(cc - kk), 0).astype(jnp.float32).astype(jnp.bfloat16)

    def body(g, carry):
        his, los = [], []
        for r in range(group):
            hi, lo = split2(src[g * group + r])
            out = jnp.dot(band_y, hi, preferred_element_type=jnp.float32) + jnp.dot(
                band_y, lo, preferred_element_type=jnp.float32
            )
            hi, lo = split2(out)
            his.append(hi)
            los.append(lo)
        both = jnp.dot(
            jnp.concatenate(his + los, 0), band_z, preferred_element_type=jnp.float32
        )
        half = group * ry
        total = both[:half] + both[half:]
        for r in range(group):
            dst[g * group + r] = total[r * ry : (r + 1) * ry]
        return carry

    lax.fori_loop(0, rows // group, body, 0)


def filter_x(src, tile, emit):
    count = src.shape[0] - 2 * RADIUS
    load = lambda i: src[i, tile, :]
    box = load(0)
    for k in range(1, SPAN):
        box = box + load(k)
    window = [box]
    for n in range(1, SPAN):
        box = box + (load(n + RADIUS) - load(n - 1))
        window.append(box)
    total = window[0]
    for k in range(1, SPAN):
        total = total + window[k]
    emit(0, total)
    for i in range(1, count):
        n = i + RADIUS
        box = box + (load(n + RADIUS) - load(n - 1))
        total = total + (box - window[i - 1])
        window.append(box)
        emit(i, total)


(DES_UP, DES_DN, MASK, SENS, AFLD, A_UP, A_DN, V_UP, V_DN, O_UP, O_DN, VB, OB,
 VY_UP, VY_DN, OY_UP, OY_DN, COUNT) = range(18)


def kernel(design, sens, mask, new_out, obj_out, lam_out, vol_out, phys_out, full_mask, dbuf, afull, abuf, mbuf,
           sbuf, vbuf, obuf, vx, ox, vback, oback, ybox, xbox, send_sems, recv_sems, local_sems, y_send, y_recv,
           x_send, x_recv):
    rows, ry, depth = design.shape
    half = depth // 2
    gx, gy = lax.axis_index("gx"), lax.axis_index("gy")
    nx, ny = lax.axis_size("gx"), lax.axis_size("gy")
    par = lax.rem(gx, 2)
    pair = gx // 2
    partner = gx + 1 - 2 * par
    has_xl, has_xr = gx >= 2, gx < nx - 2
    has_yl, has_yr = gy >= 1, gy < ny - 1
    xl, xr, yl, yr = (gx - 2, gy), (gx + 2, gy), (gx, gy - 1), (gx, gy + 1)
    mate = (partner, gy)

    barrier = pltpu.get_barrier_semaphore()

    def greet(dev):
        pl.semaphore_signal(barrier, inc=1, device_id=dev, device_id_type=MESH)

    for k in range(1, nx):
        greet((lax.rem(gx + k, nx), gy))
    for k in range(1, ny):
        greet((gx, lax.rem(gy + k, ny)))

    own = pl.ds(pl.multiple_of(par * half, 128), half)
    other = pl.ds(pl.multiple_of((1 - par) * half, 128), half)
    my_rows = pl.ds(par * rows, rows)
    mate_rows = pl.ds((1 - par) * rows, rows)
    mid = pl.ds(RADIUS, ry)

    l_des = pltpu.make_async_copy(design, dbuf.at[:, mid, :], local_sems.at[0])
    l_mask = pltpu.make_async_copy(mask.at[:, :, own], mbuf.at[my_rows], local_sems.at[1])
    l_sens = pltpu.make_async_copy(sens.at[:, :, own], sbuf.at[my_rows], local_sems.at[2])
    l_des.start()
    l_mask.start()
    l_sens.start()

    l_full = pltpu.make_async_copy(mask, full_mask, local_sems.at[6])
    l_full.start()
    pl.semaphore_wait(barrier, nx + ny - 2)

    def remote(idx, src, dst, dev):
        return pltpu.make_async_remote_copy(
            src_ref=src, dst_ref=dst, send_sem=send_sems.at[idx], recv_sem=recv_sems.at[idx],
            device_id=dev, device_id_type=MESH,
        )

    def y_pair(up, dn, src, off, buf):
        return (
            remote(up, src.at[:, pl.ds(off + ry - RADIUS, RADIUS), :], buf.at[:, pl.ds(0, RADIUS), :], yr),
            remote(dn, src.at[:, pl.ds(off, RADIUS), :], buf.at[:, pl.ds(RADIUS + ry, RADIUS), :], yl),
        )

    def x_pair(up, dn, buf):
        return (
            remote(up, buf.at[pl.ds(2 * rows, RADIUS)], buf.at[pl.ds(0, RADIUS)], xr),
            remote(dn, buf.at[pl.ds(RADIUS, RADIUS)], buf.at[pl.ds(RADIUS + 2 * rows, RADIUS)], xl),
        )

    def begin(two, low, high):
        pl.when(high)(lambda: two[0].start())
        pl.when(low)(lambda: two[1].start())

    def finish(two, low, high):
        pl.when(low)(lambda: two[0].wait_recv())
        pl.when(high)(lambda: two[1].wait_recv())

    def sent(two, low, high):
        pl.when(high)(lambda: two[0].wait_send())
        pl.when(low)(lambda: two[1].wait_send())

    r_des = y_pair(DES_UP, DES_DN, design, 0, dbuf)
    begin(r_des, has_yl, has_yr)
    r_mask = remote(MASK, mask.at[:, :, other], mbuf.at[my_rows], mate)
    r_mask.start()

    def zero_y(buf):
        zero = jnp.zeros((rows, RADIUS, depth), jnp.float32)

        @pl.when(jnp.logical_not(has_yl))
        def _():
            buf[:, 0:RADIUS, :] = zero

        @pl.when(jnp.logical_not(has_yr))
        def _():
            buf[:, RADIUS + ry :, :] = zero

    def zero_x(buf):
        zero = jnp.zeros((RADIUS, ry, half), jnp.float32)

        @pl.when(jnp.logical_not(has_xl))
        def _():
            buf[0:RADIUS] = zero

        @pl.when(jnp.logical_not(has_xr))
        def _():
            buf[RADIUS + 2 * rows :] = zero

    for buf in (dbuf, vback, oback):
        zero_y(buf)
    for buf in (abuf, vbuf, obuf):
        zero_x(buf)

    group = 4 if rows % 4 == 0 else 1
    l_des.wait()
    finish(r_des, has_yl, has_yr)
    filter_zy(dbuf, afull, group)
    r_a = remote(AFLD, afull.at[:, :, other], abuf.at[pl.ds(RADIUS + par * rows, rows)], mate)
    r_a.start()
    r_sens = remote(SENS, sens.at[:, :, other], sbuf.at[my_rows], mate)
    r_sens.start()
    l_a = pltpu.make_async_copy(afull.at[:, :, own], abuf.at[pl.ds(RADIUS + par * rows, rows)], local_sems.at[3])
    l_a.start()
    l_a.wait()
    r_a.wait_recv()
    x_a = x_pair(A_UP, A_DN, abuf)
    begin(x_a, has_xl, has_xr)
    l_mask.wait()
    r_mask.wait_recv()
    finish(x_a, has_xl, has_xr)

    total_x, total_y = rows * nx, ry * ny
    wz = cover(par * half + lax.broadcasted_iota(jnp.int32, (8, half), 1), depth)

    phys_out[...] = jnp.zeros_like(phys_out)

    def stage_one(j, carry):
        tile = pl.ds(pl.multiple_of(j * 8, 8), 8)
        wy = cover(gy * ry + j * 8 + lax.broadcasted_iota(jnp.int32, (8, half), 0), total_y)
        wyz = wy * wz

        def emit(i, value):
            weight = wyz * cover(pair * (2 * rows) + i, total_x)
            inv = 1.0 / weight
            shifted = jnp.tanh(beta_value * (value * inv - eta_value))
            solid = mbuf[i, tile, :]
            free = (1 - solid).astype(jnp.float32)
            phys_out[...] += jnp.where(solid == 1, 1.0, (TANH_MID + shifted) * (1.0 / SCALE))
            vbuf[RADIUS + i, tile, :] = (beta_value / SCALE) * (1.0 - shifted * shifted) * free * inv

        filter_x(abuf, tile, emit)
        return carry

    lax.fori_loop(0, ry // 8, stage_one, 0)
    x_v = x_pair(V_UP, V_DN, vbuf)
    begin(x_v, has_xl, has_xr)
    finish(x_v, has_xl, has_xr)

    def x_only(src, dst):
        def body(j, carry):
            tile = pl.ds(pl.multiple_of(j * 8, 8), 8)

            def emit(i, value):
                dst[i, tile, :] = value

            filter_x(src, tile, emit)
            return carry

        lax.fori_loop(0, ry // 8, body, 0)

    x_only(vbuf, vx)
    r_vb = remote(VB, vx.at[mate_rows], vback.at[:, mid, own], mate)
    r_vb.start()
    l_vb = pltpu.make_async_copy(vx.at[my_rows], vback.at[:, mid, own], local_sems.at[4])
    l_vb.start()

    l_sens.wait()
    r_sens.wait_recv()

    def times(i, carry):
        obuf[RADIUS + i] = -sbuf[i] * vbuf[RADIUS + i]
        return carry

    lax.fori_loop(0, 2 * rows, times, 0)
    x_o = x_pair(O_UP, O_DN, obuf)
    begin(x_o, has_xl, has_xr)
    finish(x_o, has_xl, has_xr)
    x_only(obuf, ox)
    r_ob = remote(OB, ox.at[mate_rows], oback.at[:, mid, own], mate)
    r_ob.start()
    l_ob = pltpu.make_async_copy(ox.at[my_rows], oback.at[:, mid, own], local_sems.at[5])
    l_ob.start()

    l_vb.wait()
    r_vb.wait_recv()
    y_v = y_pair(VY_UP, VY_DN, vback, RADIUS, vback)
    begin(y_v, has_yl, has_yr)
    finish(y_v, has_yl, has_yr)
    filter_zy(vback, vol_out, group)

    l_ob.wait()
    r_ob.wait_recv()
    y_o = y_pair(OY_UP, OY_DN, oback, RADIUS, oback)
    begin(y_o, has_yl, has_yr)
    finish(y_o, has_yl, has_yr)
    filter_zy(oback, obj_out, group)

    l_full.wait()

    def along(turn, coord, size, place, box, send, recv):
        for k in range(1, size):
            peer = lax.rem(coord + k, size)
            pltpu.make_async_remote_copy(
                src_ref=box.at[turn, coord], dst_ref=box.at[turn, coord], send_sem=send.at[turn, k],
                recv_sem=recv.at[turn, coord], device_id=place(peer), device_id_type=MESH,
            ).start()
        for k in range(1, size):
            peer = lax.rem(coord + k, size)
            pltpu.make_async_remote_copy(
                src_ref=box.at[turn, peer], dst_ref=box.at[turn, peer], send_sem=send.at[turn, k],
                recv_sem=recv.at[turn, peer], device_id=place(peer), device_id_type=MESH,
            ).wait()
        out = box[turn, 0]
        for k in range(1, size):
            out = out + box[turn, k]
        return out

    def all_sum(turn, tile):
        ybox[turn, gy] = tile
        tile = along(turn, gy, ny, lambda peer: (gx, peer), ybox, y_send, y_recv)
        xbox[turn, gx] = tile
        tile = along(turn, gx, nx, lambda peer: (peer, gy), xbox, x_send, x_recv)
        return jnp.sum(tile, axis=1, keepdims=True)

    part = 32 if ry % 32 == 0 else 8
    pieces = ry // part

    def fold(x):
        out = x[0:8]
        for k in range(1, part // 8):
            out = out + x[8 * k : 8 * (k + 1)]
        res = out[:, 0:128]
        for k in range(1, depth // 128):
            res = res + out[:, 128 * k : 128 * (k + 1)]
        return res

    def where_is(i):
        row = i // pieces
        start = pl.multiple_of(lax.rem(i, pieces) * part, 8)
        return row, pl.ds(start, part), pl.ds(RADIUS + start, part)

    def shift_of(lam, grad, swing, cell):
        up = jnp.maximum(grad, 0.0)
        down = jnp.maximum(-grad, 0.0)
        a_two = (0.25 * 1.001) * up + (0.25 * 0.001) * down + 0.25e-05 + lam * ((0.25 * 1.001) * swing)
        b_two = (0.25 * 0.001) * up + (0.25 * 1.001) * down + 0.25e-05 + lam * ((0.25 * 0.001) * swing)
        a_root, b_root = jnp.sqrt(a_two), jnp.sqrt(b_two)
        inv = 1.0 / (a_root + b_root)
        raw = (0.5 * (b_root - a_root)) * inv
        low = jnp.maximum(-cell, -move_limit)
        high = jnp.minimum(1.0 - cell, move_limit)
        return a_root, b_root, inv, raw, low, high

    def dual_pass(lam, first):
        def body(i, carry):
            row, ys, ds = where_is(i)
            swing = vol_out[row, ys, :]
            if first:
                swing = swing * (1 - full_mask[row, ys, :]).astype(jnp.float32)
                vol_out[row, ys, :] = swing
            a_root, b_root, inv, raw, low, high = shift_of(lam, obj_out[row, ys, :], swing, dbuf[row, ds, :])
            point = jnp.clip(raw, low, high)
            p_one, q_one = (0.25 * 1.001) * swing, (0.25 * 0.001) * swing
            r_up, r_low = 1.0 / (asym_gap - point), 1.0 / (asym_gap + point)
            value_p, value_q = p_one * r_up, q_one * r_low
            ratio = a_root / b_root
            moved = 0.5 * (ratio * q_one - p_one / ratio) * (inv * inv)
            change = jnp.where(
                jnp.logical_and(raw > low, raw < high), (value_p * r_up - value_q * r_low) * moved, 0.0
            )
            out = (carry[0] + fold(value_p + value_q), carry[1] + fold(change))
            if first:
                out = out + (carry[2] + fold(swing),)
            return out

        zero = jnp.zeros((8, 128), jnp.float32)
        return lax.fori_loop(0, rows * pieces, body, (zero,) * (3 if first else 2))

    cells = float(rows * ry * depth)
    cell_count = cells * nx * ny
    index = lax.broadcasted_iota(jnp.int32, (8, 128), 0)

    def pack(parts):
        out = jnp.zeros((8, 128), jnp.float32)
        for k, one in enumerate(parts):
            out = jnp.where(index == k, jnp.sum(one, axis=0, keepdims=True), out)
        return out

    lam = jnp.full((1, 1), 1.0, jnp.float32)
    offset = None
    for turn in range(DUAL_ITERS):
        parts = dual_pass(lam, turn == 0)
        if turn == 0:
            phys = phys_out[:, 0:128]
            for k in range(1, half // 128):
                phys = phys + phys_out[:, 128 * k : 128 * (k + 1)]
            base = parts[2] * (0.25 * (1.001 + 0.001) / asym_gap)
            parts = (parts[0], parts[1], phys - base - volume_share * cells / 1024.0)
        sums = all_sum(turn, pack(parts))
        if turn == 0:
            offset = sums[2:3] / cell_count
        level = sums[0:1] / cell_count + offset
        rate = sums[1:2] / cell_count
        lam = lam * jnp.exp(-level / (lam * rate - 1e-06))

    def last(i, carry):
        row, ys, ds = where_is(i)
        cell = dbuf[row, ds, :]
        raw, low, high = shift_of(lam, obj_out[row, ys, :], vol_out[row, ys, :], cell)[3:]
        point = cell + jnp.clip(raw, low, high)
        new_out[row, ys, :] = jnp.where(full_mask[row, ys, :] == 1, cell, point)
        return carry

    lax.fori_loop(0, rows * pieces, last, 0)
    lam_out[0, 0] = lam[0, 0]

    for one in (r_mask, r_a, r_sens, r_vb, r_ob):
        one.wait_send()
    for two in (r_des, y_v, y_o):
        sent(two, has_yl, has_yr)
    for two in (x_a, x_v, x_o):
        sent(two, has_xl, has_xr)


def per_device(design, sensitivity, solid_mask):
    rows, ry, depth = design.shape
    half = depth // 2
    nx, ny = lax.axis_size("gx"), lax.axis_size("gy")
    f32 = jnp.float32
    block = (rows, ry, depth)
    wide = (rows, ry + 2 * RADIUS, depth)
    tall = (2 * rows + 2 * RADIUS, ry, half)
    strip = (2 * rows, ry, half)
    vmem = pl.BlockSpec(memory_space=pltpu.VMEM)
    dma = pltpu.SemaphoreType.DMA
    new_design, objective_grad, lam = pl.pallas_call(
        kernel,
        out_shape=(
            jax.ShapeDtypeStruct(block, f32),
            jax.ShapeDtypeStruct(block, f32),
            jax.ShapeDtypeStruct((1, 1), f32),
        ),
        in_specs=[pl.BlockSpec(memory_space=pl.ANY)] * 3,
        out_specs=(vmem, vmem, pl.BlockSpec(memory_space=pltpu.SMEM)),
        scratch_shapes=[
            pltpu.VMEM(block, f32),
            pltpu.VMEM((8, half), f32),
            pltpu.VMEM(block, jnp.int32),
            pltpu.VMEM(wide, f32),
            pltpu.VMEM(block, f32),
            pltpu.VMEM(tall, f32),
            pltpu.VMEM(strip, jnp.int32),
            pltpu.VMEM(strip, f32),
            pltpu.VMEM(tall, f32),
            pltpu.VMEM(tall, f32),
            pltpu.VMEM(strip, f32),
            pltpu.VMEM(strip, f32),
            pltpu.VMEM(wide, f32),
            pltpu.VMEM(wide, f32),
            pltpu.VMEM((DUAL_ITERS, ny, 8, 128), f32),
            pltpu.VMEM((DUAL_ITERS, nx, 8, 128), f32),
            dma((COUNT,)),
            dma((COUNT,)),
            dma((7,)),
            dma((DUAL_ITERS, ny)),
            dma((DUAL_ITERS, ny)),
            dma((DUAL_ITERS, nx)),
            dma((DUAL_ITERS, nx)),
        ],
        compiler_params=pltpu.CompilerParams(
            collective_id=0, has_side_effects=True, vmem_limit_bytes=56 * 1024 * 1024
        ),
    )(design, sensitivity, solid_mask)
    return new_design, objective_grad, lam.reshape(())


def solution(mesh):
    return jax.shard_map(
        per_device,
        mesh=mesh,
        in_specs=(P("gx", "gy", None), P("gx", "gy", None), P("gx", "gy", None)),
        out_specs=(P("gx", "gy", None), P("gx", "gy", None), P()),
        check_vma=False,
    )
```

```python
import functools
import math

import jax
import jax.numpy as jnp
from jax import lax
from jax.experimental import pallas as pl
from jax.experimental.pallas import tpu as pltpu
from jax.sharding import PartitionSpec as P

RADIUS = 8
DUAL_ITERS = 2
SPAN = RADIUS + 1
MESH = pl.DeviceIdType.MESH

beta_value = 4.0
eta_value = 0.5
volume_share = 0.4
move_limit = 0.2
asym_gap = 0.5
TANH_MID = math.tanh(beta_value * eta_value)
SCALE = math.tanh(beta_value * eta_value) + math.tanh(beta_value * (1.0 - eta_value))


def missing(distance):
    out = jnp.maximum(RADIUS - distance, 0)
    return (out * (out + 1)) // 2


def cover(cell, total):
    return (SPAN * SPAN - missing(cell) - missing(total - 1 - cell)).astype(jnp.float32)


def split2(x):
    hi = x.astype(jnp.bfloat16)
    lo = (x - hi.astype(jnp.float32)).astype(jnp.bfloat16)
    return hi, lo


def filter_zy(src, dst, group, first=0, rows=None):
    _, wide, depth = src.shape
    rows = src.shape[0] if rows is None else rows
    ry = wide - 2 * RADIUS
    jj = lax.broadcasted_iota(jnp.int32, (ry, wide), 0)
    bb = lax.broadcasted_iota(jnp.int32, (ry, wide), 1)
    band_y = jnp.maximum(SPAN - jnp.abs(jj + RADIUS - bb), 0).astype(jnp.float32).astype(jnp.bfloat16)
    cc = lax.broadcasted_iota(jnp.int32, (depth, depth), 0)
    kk = lax.broadcasted_iota(jnp.int32, (depth, depth), 1)
    band_z = jnp.maximum(SPAN - jnp.abs(cc - kk), 0).astype(jnp.float32).astype(jnp.bfloat16)

    def body(g, carry):
        his, los = [], []
        for r in range(group):
            hi, lo = split2(src[first + g * group + r])
            out = jnp.dot(band_y, hi, preferred_element_type=jnp.float32) + jnp.dot(
                band_y, lo, preferred_element_type=jnp.float32
            )
            hi, lo = split2(out)
            his.append(hi)
            los.append(lo)
        both = jnp.dot(
            jnp.concatenate(his + los, 0), band_z, preferred_element_type=jnp.float32
        )
        half = group * ry
        total = both[:half] + both[half:]
        for r in range(group):
            dst[first + g * group + r] = total[r * ry : (r + 1) * ry]
        return carry

    lax.fori_loop(0, rows // group, body, 0)


def filter_x(src, tile, emit):
    count = src.shape[0] - 2 * RADIUS
    load = lambda i: src[i, tile, :]
    box = load(0)
    for k in range(1, SPAN):
        box = box + load(k)
    window = [box]
    for n in range(1, SPAN):
        box = box + (load(n + RADIUS) - load(n - 1))
        window.append(box)
    total = window[0]
    for k in range(1, SPAN):
        total = total + window[k]
    emit(0, total)
    for i in range(1, count):
        n = i + RADIUS
        box = box + (load(n + RADIUS) - load(n - 1))
        total = total + (box - window[i - 1])
        window.append(box)
        emit(i, total)


(DES_UP, DES_DN, MASK, SENS, AFLD, A_UP, A_DN, V_UP, V_DN, O_UP, O_DN, VB,
 VY_UP, VY_DN, MASK_TWO, LAST) = range(16)
CHUNKS = 4
OB, OY_UP, OY_DN, COUNT = LAST, LAST + CHUNKS, LAST + 2 * CHUNKS, LAST + 3 * CHUNKS


def kernel(design, sens, mask, new_out, obj_out, lam_out, vol_out, phys_out, full_mask, dbuf, afull, abuf, mbuf,
           sbuf, vbuf, obuf, vx, ox, vback, oback, ybox, xbox, send_sems, recv_sems, local_sems, y_send, y_recv,
           x_send, x_recv):
    rows, ry, depth = design.shape
    half = depth // 2
    gx, gy = lax.axis_index("gx"), lax.axis_index("gy")
    nx, ny = lax.axis_size("gx"), lax.axis_size("gy")
    par = lax.rem(gx, 2)
    pair = gx // 2
    partner = gx + 1 - 2 * par
    has_xl, has_xr = gx >= 2, gx < nx - 2
    has_yl, has_yr = gy >= 1, gy < ny - 1
    xl, xr, yl, yr = (gx - 2, gy), (gx + 2, gy), (gx, gy - 1), (gx, gy + 1)
    mate = (partner, gy)

    barrier = pltpu.get_barrier_semaphore()

    def greet(dev):
        pl.semaphore_signal(barrier, inc=1, device_id=dev, device_id_type=MESH)

    for k in range(1, nx):
        greet((lax.rem(gx + k, nx), gy))
    for k in range(1, ny):
        greet((gx, lax.rem(gy + k, ny)))

    own = pl.ds(pl.multiple_of(par * half, 128), half)
    other = pl.ds(pl.multiple_of((1 - par) * half, 128), half)
    my_rows = pl.ds(par * rows, rows)
    mate_rows = pl.ds((1 - par) * rows, rows)
    mid = pl.ds(RADIUS, ry)

    l_des = pltpu.make_async_copy(design, dbuf.at[:, mid, :], local_sems.at[0])
    l_mask = pltpu.make_async_copy(mask.at[:, :, own], mbuf.at[my_rows], local_sems.at[1])
    l_sens = pltpu.make_async_copy(sens.at[:, :, own], sbuf.at[my_rows], local_sems.at[2])
    l_des.start()
    l_mask.start()
    l_sens.start()

    l_full = pltpu.make_async_copy(mask, full_mask, local_sems.at[6])
    l_full.start()
    pl.semaphore_wait(barrier, nx + ny - 2)

    def remote(idx, src, dst, dev):
        return pltpu.make_async_remote_copy(
            src_ref=src, dst_ref=dst, send_sem=send_sems.at[idx], recv_sem=recv_sems.at[idx],
            device_id=dev, device_id_type=MESH,
        )

    def y_pair(up, dn, src, off, buf):
        return (
            remote(up, src.at[:, pl.ds(off + ry - RADIUS, RADIUS), :], buf.at[:, pl.ds(0, RADIUS), :], yr),
            remote(dn, src.at[:, pl.ds(off, RADIUS), :], buf.at[:, pl.ds(RADIUS + ry, RADIUS), :], yl),
        )

    def x_pair(up, dn, buf):
        return (
            remote(up, buf.at[pl.ds(2 * rows, RADIUS)], buf.at[pl.ds(0, RADIUS)], xr),
            remote(dn, buf.at[pl.ds(RADIUS, RADIUS)], buf.at[pl.ds(RADIUS + 2 * rows, RADIUS)], xl),
        )

    def begin(two, low, high):
        pl.when(high)(lambda: two[0].start())
        pl.when(low)(lambda: two[1].start())

    def finish(two, low, high):
        pl.when(low)(lambda: two[0].wait_recv())
        pl.when(high)(lambda: two[1].wait_recv())

    def sent(two, low, high):
        pl.when(high)(lambda: two[0].wait_send())
        pl.when(low)(lambda: two[1].wait_send())

    r_des = y_pair(DES_UP, DES_DN, design, 0, dbuf)
    begin(r_des, has_yl, has_yr)
    ahead = max(rows // 4, 1)
    r_mask = remote(MASK, mask.at[pl.ds(0, ahead), :, other], mbuf.at[pl.ds(par * rows, ahead)], mate)
    r_mask.start()
    r_rest = remote(
        MASK_TWO, mask.at[pl.ds(ahead, rows - ahead), :, other],
        mbuf.at[pl.ds(par * rows + ahead, rows - ahead)], mate,
    )

    def zero_y(buf):
        zero = jnp.zeros((rows, RADIUS, depth), jnp.float32)

        @pl.when(jnp.logical_not(has_yl))
        def _():
            buf[:, 0:RADIUS, :] = zero

        @pl.when(jnp.logical_not(has_yr))
        def _():
            buf[:, RADIUS + ry :, :] = zero

    def zero_x(buf):
        zero = jnp.zeros((RADIUS, ry, half), jnp.float32)

        @pl.when(jnp.logical_not(has_xl))
        def _():
            buf[0:RADIUS] = zero

        @pl.when(jnp.logical_not(has_xr))
        def _():
            buf[RADIUS + 2 * rows :] = zero

    for buf in (dbuf, vback, oback):
        zero_y(buf)
    for buf in (abuf, vbuf, obuf):
        zero_x(buf)

    group = 4 if rows % 4 == 0 else 1
    l_des.wait()
    finish(r_des, has_yl, has_yr)
    filter_zy(dbuf, afull, group)
    r_a = remote(AFLD, afull.at[:, :, other], abuf.at[pl.ds(RADIUS + par * rows, rows)], mate)
    r_a.start()
    r_rest.start()
    r_sens = remote(SENS, sens.at[:, :, other], sbuf.at[my_rows], mate)
    r_sens.start()
    l_a = pltpu.make_async_copy(afull.at[:, :, own], abuf.at[pl.ds(RADIUS + par * rows, rows)], local_sems.at[3])
    l_a.start()
    l_a.wait()
    r_a.wait_recv()
    x_a = x_pair(A_UP, A_DN, abuf)
    begin(x_a, has_xl, has_xr)
    l_mask.wait()
    r_mask.wait_recv()
    r_rest.wait_recv()
    finish(x_a, has_xl, has_xr)

    total_x, total_y = rows * nx, ry * ny
    wz = cover(par * half + lax.broadcasted_iota(jnp.int32, (8, half), 1), depth)

    phys_out[...] = jnp.zeros_like(phys_out)

    def stage_one(j, carry):
        tile = pl.ds(pl.multiple_of(j * 8, 8), 8)
        wy = cover(gy * ry + j * 8 + lax.broadcasted_iota(jnp.int32, (8, half), 0), total_y)
        wyz = wy * wz

        def emit(i, value):
            weight = wyz * cover(pair * (2 * rows) + i, total_x)
            inv = 1.0 / weight
            shifted = jnp.tanh(beta_value * (value * inv - eta_value))
            solid = mbuf[i, tile, :]
            free = (1 - solid).astype(jnp.float32)
            phys_out[...] += jnp.where(solid == 1, 1.0, (TANH_MID + shifted) * (1.0 / SCALE))
            vbuf[RADIUS + i, tile, :] = (beta_value / SCALE) * (1.0 - shifted * shifted) * free * inv

        filter_x(abuf, tile, emit)
        return carry

    lax.fori_loop(0, ry // 8, stage_one, 0)
    x_v = x_pair(V_UP, V_DN, vbuf)
    begin(x_v, has_xl, has_xr)
    finish(x_v, has_xl, has_xr)

    def x_only(src, dst):
        def body(j, carry):
            tile = pl.ds(pl.multiple_of(j * 8, 8), 8)

            def emit(i, value):
                dst[i, tile, :] = value

            filter_x(src, tile, emit)
            return carry

        lax.fori_loop(0, ry // 8, body, 0)

    x_only(vbuf, vx)
    r_vb = remote(VB, vx.at[mate_rows], vback.at[:, mid, own], mate)
    r_vb.start()
    l_vb = pltpu.make_async_copy(vx.at[my_rows], vback.at[:, mid, own], local_sems.at[4])
    l_vb.start()

    l_sens.wait()
    r_sens.wait_recv()

    def times(i, carry):
        obuf[RADIUS + i] = -sbuf[i] * vbuf[RADIUS + i]
        return carry

    lax.fori_loop(0, 2 * rows, times, 0)
    x_o = x_pair(O_UP, O_DN, obuf)
    begin(x_o, has_xl, has_xr)
    finish(x_o, has_xl, has_xr)
    x_only(obuf, ox)
    chunks = CHUNKS if rows % CHUNKS == 0 else 1
    step = rows // chunks
    r_ob = [
        remote(OB + c, ox.at[pl.ds((1 - par) * rows + c * step, step)],
               oback.at[pl.ds(c * step, step), mid, own], mate)
        for c in range(chunks)
    ]
    for one in r_ob:
        one.start()
    l_ob = pltpu.make_async_copy(ox.at[my_rows], oback.at[:, mid, own], local_sems.at[5])
    l_ob.start()

    l_vb.wait()
    r_vb.wait_recv()
    y_v = y_pair(VY_UP, VY_DN, vback, RADIUS, vback)
    begin(y_v, has_yl, has_yr)
    finish(y_v, has_yl, has_yr)
    filter_zy(vback, vol_out, group)

    l_full.wait()

    def along(turn, coord, size, place, box, send, recv):
        for k in range(1, size):
            peer = lax.rem(coord + k, size)
            pltpu.make_async_remote_copy(
                src_ref=box.at[turn, coord], dst_ref=box.at[turn, coord], send_sem=send.at[turn, k],
                recv_sem=recv.at[turn, coord], device_id=place(peer), device_id_type=MESH,
            ).start()
        for k in range(1, size):
            peer = lax.rem(coord + k, size)
            pltpu.make_async_remote_copy(
                src_ref=box.at[turn, peer], dst_ref=box.at[turn, peer], send_sem=send.at[turn, k],
                recv_sem=recv.at[turn, peer], device_id=place(peer), device_id_type=MESH,
            ).wait()
        out = box[turn, 0]
        for k in range(1, size):
            out = out + box[turn, k]
        return out

    def all_sum(turn, tile):
        ybox[turn, gy] = tile
        tile = along(turn, gy, ny, lambda peer: (gx, peer), ybox, y_send, y_recv)
        xbox[turn, gx] = tile
        tile = along(turn, gx, nx, lambda peer: (peer, gy), xbox, x_send, x_recv)
        return jnp.sum(tile, axis=1, keepdims=True)

    part = 32 if ry % 32 == 0 else 8
    pieces = ry // part

    def fold(x):
        out = x[0:8]
        for k in range(1, part // 8):
            out = out + x[8 * k : 8 * (k + 1)]
        res = out[:, 0:128]
        for k in range(1, depth // 128):
            res = res + out[:, 128 * k : 128 * (k + 1)]
        return res

    def where_is(i):
        row = i // pieces
        start = pl.multiple_of(lax.rem(i, pieces) * part, 8)
        return row, pl.ds(start, part), pl.ds(RADIUS + start, part)

    def shift_of(lam, grad, swing, cell):
        up = jnp.maximum(grad, 0.0)
        down = jnp.maximum(-grad, 0.0)
        a_two = (0.25 * 1.001) * up + (0.25 * 0.001) * down + 0.25e-05 + lam * ((0.25 * 1.001) * swing)
        b_two = (0.25 * 0.001) * up + (0.25 * 1.001) * down + 0.25e-05 + lam * ((0.25 * 0.001) * swing)
        a_inv, b_inv = lax.rsqrt(a_two), lax.rsqrt(b_two)
        a_root, b_root = a_two * a_inv, b_two * b_inv
        inv = pl.reciprocal(a_root + b_root)
        raw = (0.5 * (b_root - a_root)) * inv
        low = jnp.maximum(-cell, -move_limit)
        high = jnp.minimum(1.0 - cell, move_limit)
        return a_root, b_root, a_inv, b_inv, inv, raw, low, high

    def dual_pass(lam, first, begin_at, number, start):
        def body(i, carry):
            row, ys, ds = where_is(i)
            swing = vol_out[row, ys, :]
            if first:
                swing = swing * (1 - full_mask[row, ys, :]).astype(jnp.float32)
                vol_out[row, ys, :] = swing
            a_root, b_root, a_inv, b_inv, inv, raw, low, high = shift_of(
                lam, obj_out[row, ys, :], swing, dbuf[row, ds, :]
            )
            point = jnp.clip(raw, low, high)
            p_one, q_one = (0.25 * 1.001) * swing, (0.25 * 0.001) * swing
            both = pl.reciprocal(asym_gap * asym_gap - point * point)
            r_up, r_low = (asym_gap + point) * both, (asym_gap - point) * both
            value_p, value_q = p_one * r_up, q_one * r_low
            moved = 0.5 * (a_root * b_inv * q_one - b_root * a_inv * p_one) * (inv * inv)
            change = jnp.where(
                jnp.logical_and(raw > low, raw < high), (value_p * r_up - value_q * r_low) * moved, 0.0
            )
            out = (carry[0] + fold(value_p + value_q), carry[1] + fold(change))
            if first:
                out = out + (carry[2] + fold(swing),)
            return out

        return lax.fori_loop(begin_at * pieces, (begin_at + number) * pieces, body, start)

    cells = float(rows * ry * depth)
    cell_count = cells * nx * ny
    index = lax.broadcasted_iota(jnp.int32, (8, 128), 0)

    def pack(parts):
        out = jnp.zeros((8, 128), jnp.float32)
        for k, one in enumerate(parts):
            out = jnp.where(index == k, jnp.sum(one, axis=0, keepdims=True), out)
        return out

    lam = jnp.full((1, 1), 1.0, jnp.float32)
    offset = None
    zero = jnp.zeros((8, 128), jnp.float32)

    l_ob.wait()
    y_o = []
    parts = (zero,) * 3
    for c in range(chunks + 1):
        if c < chunks:
            r_ob[c].wait_recv()
            piece = oback.at[pl.ds(c * step, step)]
            y_o.append(y_pair(OY_UP + c, OY_DN + c, piece, RADIUS, piece))
            begin(y_o[c], has_yl, has_yr)
        if c >= 1:
            finish(y_o[c - 1], has_yl, has_yr)
            filter_zy(oback, obj_out, step, (c - 1) * step, step)
            parts = dual_pass(lam, True, (c - 1) * step, step, parts)

    for turn in range(DUAL_ITERS):
        if turn > 0:
            parts = dual_pass(lam, False, 0, rows, (zero,) * 2)
        if turn == 0:
            phys = phys_out[:, 0:128]
            for k in range(1, half // 128):
                phys = phys + phys_out[:, 128 * k : 128 * (k + 1)]
            base = parts[2] * (0.25 * (1.001 + 0.001) / asym_gap)
            parts = (parts[0], parts[1], phys - base - volume_share * cells / 1024.0)
        sums = all_sum(turn, pack(parts))
        if turn == 0:
            offset = sums[2:3] / cell_count
        level = sums[0:1] / cell_count + offset
        rate = sums[1:2] / cell_count
        lam = lam * jnp.exp(-level / (lam * rate - 1e-06))

    def last(i, carry):
        row, ys, ds = where_is(i)
        cell = dbuf[row, ds, :]
        raw, low, high = shift_of(lam, obj_out[row, ys, :], vol_out[row, ys, :], cell)[5:]
        point = cell + jnp.clip(raw, low, high)
        new_out[row, ys, :] = jnp.where(full_mask[row, ys, :] == 1, cell, point)
        return carry

    lax.fori_loop(0, rows * pieces, last, 0)
    lam_out[0, 0] = lam[0, 0]

    for one in (r_mask, r_rest, r_a, r_sens, r_vb, *r_ob):
        one.wait_send()
    for two in (r_des, y_v, *y_o):
        sent(two, has_yl, has_yr)
    for two in (x_a, x_v, x_o):
        sent(two, has_xl, has_xr)


def per_device(design, sensitivity, solid_mask):
    rows, ry, depth = design.shape
    half = depth // 2
    nx, ny = lax.axis_size("gx"), lax.axis_size("gy")
    f32 = jnp.float32
    block = (rows, ry, depth)
    wide = (rows, ry + 2 * RADIUS, depth)
    tall = (2 * rows + 2 * RADIUS, ry, half)
    strip = (2 * rows, ry, half)
    vmem = pl.BlockSpec(memory_space=pltpu.VMEM)
    dma = pltpu.SemaphoreType.DMA
    new_design, objective_grad, lam = pl.pallas_call(
        kernel,
        out_shape=(
            jax.ShapeDtypeStruct(block, f32),
            jax.ShapeDtypeStruct(block, f32),
            jax.ShapeDtypeStruct((1, 1), f32),
        ),
        in_specs=[pl.BlockSpec(memory_space=pl.ANY)] * 3,
        out_specs=(vmem, vmem, pl.BlockSpec(memory_space=pltpu.SMEM)),
        scratch_shapes=[
            pltpu.VMEM(block, f32),
            pltpu.VMEM((8, half), f32),
            pltpu.VMEM(block, jnp.int32),
            pltpu.VMEM(wide, f32),
            pltpu.VMEM(block, f32),
            pltpu.VMEM(tall, f32),
            pltpu.VMEM(strip, jnp.int32),
            pltpu.VMEM(strip, f32),
            pltpu.VMEM(tall, f32),
            pltpu.VMEM(tall, f32),
            pltpu.VMEM(strip, f32),
            pltpu.VMEM(strip, f32),
            pltpu.VMEM(wide, f32),
            pltpu.VMEM(wide, f32),
            pltpu.VMEM((DUAL_ITERS, ny, 8, 128), f32),
            pltpu.VMEM((DUAL_ITERS, nx, 8, 128), f32),
            dma((COUNT,)),
            dma((COUNT,)),
            dma((7,)),
            dma((DUAL_ITERS, ny)),
            dma((DUAL_ITERS, ny)),
            dma((DUAL_ITERS, nx)),
            dma((DUAL_ITERS, nx)),
        ],
        compiler_params=pltpu.CompilerParams(
            collective_id=0, has_side_effects=True, vmem_limit_bytes=56 * 1024 * 1024
        ),
    )(design, sensitivity, solid_mask)
    return new_design, objective_grad, lam.reshape(())


def solution(mesh):
    return jax.shard_map(
        per_device,
        mesh=mesh,
        in_specs=(P("gx", "gy", None), P("gx", "gy", None), P("gx", "gy", None)),
        out_specs=(P("gx", "gy", None), P("gx", "gy", None), P()),
        check_vma=False,
    )
```

```python
import functools
import math

import jax
import jax.numpy as jnp
from jax import lax
from jax.experimental import pallas as pl
from jax.experimental.pallas import tpu as pltpu
from jax.sharding import PartitionSpec as P

RADIUS = 8
DUAL_ITERS = 2
SPAN = RADIUS + 1
MESH = pl.DeviceIdType.MESH

beta_value = 4.0
eta_value = 0.5
volume_share = 0.4
move_limit = 0.2
asym_gap = 0.5
TANH_MID = math.tanh(beta_value * eta_value)
SCALE = math.tanh(beta_value * eta_value) + math.tanh(beta_value * (1.0 - eta_value))


def missing(distance):
    out = jnp.maximum(RADIUS - distance, 0)
    return (out * (out + 1)) // 2


def cover(cell, total):
    return (SPAN * SPAN - missing(cell) - missing(total - 1 - cell)).astype(jnp.float32)


def split2(x):
    hi = x.astype(jnp.bfloat16)
    lo = (x - hi.astype(jnp.float32)).astype(jnp.bfloat16)
    return hi, lo


def filter_zy(src, dst, group, first=0, rows=None):
    _, wide, depth = src.shape
    rows = src.shape[0] if rows is None else rows
    ry = wide - 2 * RADIUS
    jj = lax.broadcasted_iota(jnp.int32, (ry, wide), 0)
    bb = lax.broadcasted_iota(jnp.int32, (ry, wide), 1)
    band_y = jnp.maximum(SPAN - jnp.abs(jj + RADIUS - bb), 0).astype(jnp.float32).astype(jnp.bfloat16)
    cc = lax.broadcasted_iota(jnp.int32, (depth, depth), 0)
    kk = lax.broadcasted_iota(jnp.int32, (depth, depth), 1)
    band_z = jnp.maximum(SPAN - jnp.abs(cc - kk), 0).astype(jnp.float32).astype(jnp.bfloat16)

    def body(g, carry):
        his, los = [], []
        for r in range(group):
            hi, lo = split2(src[first + g * group + r])
            out = jnp.dot(band_y, hi, preferred_element_type=jnp.float32) + jnp.dot(
                band_y, lo, preferred_element_type=jnp.float32
            )
            hi, lo = split2(out)
            his.append(hi)
            los.append(lo)
        both = jnp.dot(
            jnp.concatenate(his + los, 0), band_z, preferred_element_type=jnp.float32
        )
        half = group * ry
        total = both[:half] + both[half:]
        for r in range(group):
            dst[first + g * group + r] = total[r * ry : (r + 1) * ry]
        return carry

    lax.fori_loop(0, rows // group, body, 0)


def filter_x(src, tile, emit):
    count = src.shape[0] - 2 * RADIUS
    load = lambda i: src[i, tile, :]
    box = load(0)
    for k in range(1, SPAN):
        box = box + load(k)
    window = [box]
    for n in range(1, SPAN):
        box = box + (load(n + RADIUS) - load(n - 1))
        window.append(box)
    total = window[0]
    for k in range(1, SPAN):
        total = total + window[k]
    emit(0, total)
    for i in range(1, count):
        n = i + RADIUS
        box = box + (load(n + RADIUS) - load(n - 1))
        total = total + (box - window[i - 1])
        window.append(box)
        emit(i, total)


(DES_UP, DES_DN, MASK, SENS, AFLD, A_UP, A_DN, V_UP, V_DN, O_UP, O_DN, VB,
 VY_UP, VY_DN, MASK_TWO, LAST) = range(16)
CHUNKS = 8
OB, OY_UP, OY_DN, COUNT = LAST, LAST + CHUNKS, LAST + 2 * CHUNKS, LAST + 3 * CHUNKS


def kernel(design, sens, mask, new_hbm, obj_hbm, lam_out, new_out, obj_out, vol_out, phys_out, full_mask, dbuf, afull, abuf, mbuf,
           sbuf, vbuf, obuf, vx, ox, vback, oback, ybox, xbox, send_sems, recv_sems, local_sems, y_send, y_recv,
           x_send, x_recv, obj_sems, new_sems):
    rows, ry, depth = design.shape
    half = depth // 2
    gx, gy = lax.axis_index("gx"), lax.axis_index("gy")
    nx, ny = lax.axis_size("gx"), lax.axis_size("gy")
    par = lax.rem(gx, 2)
    pair = gx // 2
    partner = gx + 1 - 2 * par
    has_xl, has_xr = gx >= 2, gx < nx - 2
    has_yl, has_yr = gy >= 1, gy < ny - 1
    xl, xr, yl, yr = (gx - 2, gy), (gx + 2, gy), (gx, gy - 1), (gx, gy + 1)
    mate = (partner, gy)

    barrier = pltpu.get_barrier_semaphore()

    def greet(dev):
        pl.semaphore_signal(barrier, inc=1, device_id=dev, device_id_type=MESH)

    for k in range(1, nx):
        greet((lax.rem(gx + k, nx), gy))
    for k in range(1, ny):
        greet((gx, lax.rem(gy + k, ny)))

    own = pl.ds(pl.multiple_of(par * half, 128), half)
    other = pl.ds(pl.multiple_of((1 - par) * half, 128), half)
    my_rows = pl.ds(par * rows, rows)
    mate_rows = pl.ds((1 - par) * rows, rows)
    mid = pl.ds(RADIUS, ry)

    l_des = pltpu.make_async_copy(design, dbuf.at[:, mid, :], local_sems.at[0])
    l_mask = pltpu.make_async_copy(mask.at[:, :, own], mbuf.at[my_rows], local_sems.at[1])
    l_sens = pltpu.make_async_copy(sens.at[:, :, own], sbuf.at[my_rows], local_sems.at[2])
    l_des.start()
    l_mask.start()
    l_sens.start()

    l_full = pltpu.make_async_copy(mask, full_mask, local_sems.at[6])
    l_full.start()
    pl.semaphore_wait(barrier, nx + ny - 2)

    def remote(idx, src, dst, dev):
        return pltpu.make_async_remote_copy(
            src_ref=src, dst_ref=dst, send_sem=send_sems.at[idx], recv_sem=recv_sems.at[idx],
            device_id=dev, device_id_type=MESH,
        )

    def y_pair(up, dn, src, off, buf):
        return (
            remote(up, src.at[:, pl.ds(off + ry - RADIUS, RADIUS), :], buf.at[:, pl.ds(0, RADIUS), :], yr),
            remote(dn, src.at[:, pl.ds(off, RADIUS), :], buf.at[:, pl.ds(RADIUS + ry, RADIUS), :], yl),
        )

    def x_pair(up, dn, buf):
        return (
            remote(up, buf.at[pl.ds(2 * rows, RADIUS)], buf.at[pl.ds(0, RADIUS)], xr),
            remote(dn, buf.at[pl.ds(RADIUS, RADIUS)], buf.at[pl.ds(RADIUS + 2 * rows, RADIUS)], xl),
        )

    def begin(two, low, high):
        pl.when(high)(lambda: two[0].start())
        pl.when(low)(lambda: two[1].start())

    def finish(two, low, high):
        pl.when(low)(lambda: two[0].wait_recv())
        pl.when(high)(lambda: two[1].wait_recv())

    def sent(two, low, high):
        pl.when(high)(lambda: two[0].wait_send())
        pl.when(low)(lambda: two[1].wait_send())

    r_des = y_pair(DES_UP, DES_DN, design, 0, dbuf)
    begin(r_des, has_yl, has_yr)
    ahead = max(rows // 2, 1)
    r_mask = remote(MASK, mask.at[pl.ds(0, ahead), :, other], mbuf.at[pl.ds(par * rows, ahead)], mate)
    r_mask.start()
    r_rest = remote(
        MASK_TWO, mask.at[pl.ds(ahead, rows - ahead), :, other],
        mbuf.at[pl.ds(par * rows + ahead, rows - ahead)], mate,
    )

    def zero_y(buf):
        zero = jnp.zeros((rows, RADIUS, depth), jnp.float32)

        @pl.when(jnp.logical_not(has_yl))
        def _():
            buf[:, 0:RADIUS, :] = zero

        @pl.when(jnp.logical_not(has_yr))
        def _():
            buf[:, RADIUS + ry :, :] = zero

    def zero_x(buf):
        zero = jnp.zeros((RADIUS, ry, half), jnp.float32)

        @pl.when(jnp.logical_not(has_xl))
        def _():
            buf[0:RADIUS] = zero

        @pl.when(jnp.logical_not(has_xr))
        def _():
            buf[RADIUS + 2 * rows :] = zero

    for buf in (dbuf, vback, oback):
        zero_y(buf)
    for buf in (abuf, vbuf, obuf):
        zero_x(buf)

    group = 4 if rows % 4 == 0 else 1
    l_des.wait()
    finish(r_des, has_yl, has_yr)
    filter_zy(dbuf, afull, group)
    r_a = remote(AFLD, afull.at[:, :, other], abuf.at[pl.ds(RADIUS + par * rows, rows)], mate)
    r_a.start()
    r_rest.start()
    r_sens = remote(SENS, sens.at[:, :, other], sbuf.at[my_rows], mate)
    r_sens.start()
    l_a = pltpu.make_async_copy(afull.at[:, :, own], abuf.at[pl.ds(RADIUS + par * rows, rows)], local_sems.at[3])
    l_a.start()
    l_a.wait()
    r_a.wait_recv()
    x_a = x_pair(A_UP, A_DN, abuf)
    begin(x_a, has_xl, has_xr)
    l_mask.wait()
    r_mask.wait_recv()
    r_rest.wait_recv()
    finish(x_a, has_xl, has_xr)

    total_x, total_y = rows * nx, ry * ny
    wz = cover(par * half + lax.broadcasted_iota(jnp.int32, (8, half), 1), depth)

    phys_out[...] = jnp.zeros_like(phys_out)

    def stage_one(j, carry):
        tile = pl.ds(pl.multiple_of(j * 8, 8), 8)
        wy = cover(gy * ry + j * 8 + lax.broadcasted_iota(jnp.int32, (8, half), 0), total_y)
        wyz = wy * wz

        def emit(i, value):
            weight = wyz * cover(pair * (2 * rows) + i, total_x)
            inv = 1.0 / weight
            shifted = jnp.tanh(beta_value * (value * inv - eta_value))
            solid = mbuf[i, tile, :]
            free = (1 - solid).astype(jnp.float32)
            phys_out[...] += jnp.where(solid == 1, 1.0, (TANH_MID + shifted) * (1.0 / SCALE))
            vbuf[RADIUS + i, tile, :] = (beta_value / SCALE) * (1.0 - shifted * shifted) * free * inv

        filter_x(abuf, tile, emit)
        return carry

    lax.fori_loop(0, ry // 8, stage_one, 0)
    x_v = x_pair(V_UP, V_DN, vbuf)
    begin(x_v, has_xl, has_xr)
    finish(x_v, has_xl, has_xr)

    def x_only(src, dst):
        def body(j, carry):
            tile = pl.ds(pl.multiple_of(j * 8, 8), 8)

            def emit(i, value):
                dst[i, tile, :] = value

            filter_x(src, tile, emit)
            return carry

        lax.fori_loop(0, ry // 8, body, 0)

    x_only(vbuf, vx)
    r_vb = remote(VB, vx.at[mate_rows], vback.at[:, mid, own], mate)
    r_vb.start()
    l_vb = pltpu.make_async_copy(vx.at[my_rows], vback.at[:, mid, own], local_sems.at[4])
    l_vb.start()

    l_sens.wait()
    r_sens.wait_recv()

    def times(i, carry):
        obuf[RADIUS + i] = -sbuf[i] * vbuf[RADIUS + i]
        return carry

    lax.fori_loop(0, 2 * rows, times, 0)
    x_o = x_pair(O_UP, O_DN, obuf)
    begin(x_o, has_xl, has_xr)
    finish(x_o, has_xl, has_xr)
    x_only(obuf, ox)
    chunks = CHUNKS if rows % CHUNKS == 0 else 1
    step = rows // chunks
    r_ob = [
        remote(OB + c, ox.at[pl.ds((1 - par) * rows + c * step, step)],
               oback.at[pl.ds(c * step, step), mid, own], mate)
        for c in range(chunks)
    ]
    for one in r_ob:
        one.start()
    l_ob = pltpu.make_async_copy(ox.at[my_rows], oback.at[:, mid, own], local_sems.at[5])
    l_ob.start()

    l_vb.wait()
    r_vb.wait_recv()
    y_v = y_pair(VY_UP, VY_DN, vback, RADIUS, vback)
    begin(y_v, has_yl, has_yr)
    finish(y_v, has_yl, has_yr)
    filter_zy(vback, vol_out, group)

    l_full.wait()

    def along(turn, coord, size, place, box, send, recv):
        for k in range(1, size):
            peer = lax.rem(coord + k, size)
            pltpu.make_async_remote_copy(
                src_ref=box.at[turn, coord], dst_ref=box.at[turn, coord], send_sem=send.at[turn, k],
                recv_sem=recv.at[turn, coord], device_id=place(peer), device_id_type=MESH,
            ).start()
        for k in range(1, size):
            peer = lax.rem(coord + k, size)
            pltpu.make_async_remote_copy(
                src_ref=box.at[turn, peer], dst_ref=box.at[turn, peer], send_sem=send.at[turn, k],
                recv_sem=recv.at[turn, peer], device_id=place(peer), device_id_type=MESH,
            ).wait()
        out = box[turn, 0]
        for k in range(1, size):
            out = out + box[turn, k]
        return out

    def all_sum(turn, tile):
        ybox[turn, gy] = tile
        tile = along(turn, gy, ny, lambda peer: (gx, peer), ybox, y_send, y_recv)
        xbox[turn, gx] = tile
        tile = along(turn, gx, nx, lambda peer: (peer, gy), xbox, x_send, x_recv)
        return jnp.sum(tile, axis=1, keepdims=True)

    part = 32 if ry % 32 == 0 else 8
    pieces = ry // part

    def fold(x):
        out = x[0:8]
        for k in range(1, part // 8):
            out = out + x[8 * k : 8 * (k + 1)]
        res = out[:, 0:128]
        for k in range(1, depth // 128):
            res = res + out[:, 128 * k : 128 * (k + 1)]
        return res

    def leave(src, dst, sems, c):
        some = pl.ds(c * step, step)
        return pltpu.make_async_copy(src.at[some], dst.at[some], sems.at[c])

    def where_is(i):
        row = i // pieces
        start = pl.multiple_of(lax.rem(i, pieces) * part, 8)
        return row, pl.ds(start, part), pl.ds(RADIUS + start, part)

    def shift_of(lam, grad, swing, cell):
        up = jnp.maximum(grad, 0.0)
        down = jnp.maximum(-grad, 0.0)
        a_two = (0.25 * 1.001) * up + (0.25 * 0.001) * down + 0.25e-05 + lam * ((0.25 * 1.001) * swing)
        b_two = (0.25 * 0.001) * up + (0.25 * 1.001) * down + 0.25e-05 + lam * ((0.25 * 0.001) * swing)
        a_inv, b_inv = lax.rsqrt(a_two), lax.rsqrt(b_two)
        a_root, b_root = a_two * a_inv, b_two * b_inv
        inv = pl.reciprocal(a_root + b_root)
        raw = (0.5 * (b_root - a_root)) * inv
        low = jnp.maximum(-cell, -move_limit)
        high = jnp.minimum(1.0 - cell, move_limit)
        return a_root, b_root, a_inv, b_inv, inv, raw, low, high

    def dual_pass(lam, first, begin_at, number, start):
        def body(i, carry):
            row, ys, ds = where_is(i)
            swing = vol_out[row, ys, :]
            if first:
                swing = swing * (1 - full_mask[row, ys, :]).astype(jnp.float32)
                vol_out[row, ys, :] = swing
            a_root, b_root, a_inv, b_inv, inv, raw, low, high = shift_of(
                lam, obj_out[row, ys, :], swing, dbuf[row, ds, :]
            )
            point = jnp.clip(raw, low, high)
            p_one, q_one = (0.25 * 1.001) * swing, (0.25 * 0.001) * swing
            both = pl.reciprocal(asym_gap * asym_gap - point * point)
            r_up, r_low = (asym_gap + point) * both, (asym_gap - point) * both
            value_p, value_q = p_one * r_up, q_one * r_low
            moved = 0.5 * (a_root * b_inv * q_one - b_root * a_inv * p_one) * (inv * inv)
            change = jnp.where(
                jnp.logical_and(raw > low, raw < high), (value_p * r_up - value_q * r_low) * moved, 0.0
            )
            out = (carry[0] + fold(value_p + value_q), carry[1] + fold(change))
            if first:
                out = out + (carry[2] + fold(swing),)
            return out

        return lax.fori_loop(begin_at * pieces, (begin_at + number) * pieces, body, start)

    cells = float(rows * ry * depth)
    cell_count = cells * nx * ny
    index = lax.broadcasted_iota(jnp.int32, (8, 128), 0)

    def pack(parts):
        out = jnp.zeros((8, 128), jnp.float32)
        for k, one in enumerate(parts):
            out = jnp.where(index == k, jnp.sum(one, axis=0, keepdims=True), out)
        return out

    lam = jnp.full((1, 1), 1.0, jnp.float32)
    offset = None
    zero = jnp.zeros((8, 128), jnp.float32)

    l_ob.wait()
    y_o = []
    parts = (zero,) * 3
    for c in range(chunks + 1):
        if c < chunks:
            r_ob[c].wait_recv()
            piece = oback.at[pl.ds(c * step, step)]
            y_o.append(y_pair(OY_UP + c, OY_DN + c, piece, RADIUS, piece))
            begin(y_o[c], has_yl, has_yr)
        if c >= 1:
            finish(y_o[c - 1], has_yl, has_yr)
            filter_zy(oback, obj_out, step, (c - 1) * step, step)
            leave(obj_out, obj_hbm, obj_sems, c - 1).start()
            parts = dual_pass(lam, True, (c - 1) * step, step, parts)

    for turn in range(DUAL_ITERS):
        if turn > 0:
            parts = dual_pass(lam, False, 0, rows, (zero,) * 2)
        if turn == 0:
            phys = phys_out[:, 0:128]
            for k in range(1, half // 128):
                phys = phys + phys_out[:, 128 * k : 128 * (k + 1)]
            base = parts[2] * (0.25 * (1.001 + 0.001) / asym_gap)
            parts = (parts[0], parts[1], phys - base - volume_share * cells / 1024.0)
        sums = all_sum(turn, pack(parts))
        if turn == 0:
            offset = sums[2:3] / cell_count
        level = sums[0:1] / cell_count + offset
        rate = sums[1:2] / cell_count
        lam = lam * jnp.exp(-level / (lam * rate - 1e-06))

    def last(i, carry):
        row, ys, ds = where_is(i)
        cell = dbuf[row, ds, :]
        raw, low, high = shift_of(lam, obj_out[row, ys, :], vol_out[row, ys, :], cell)[5:]
        point = cell + jnp.clip(raw, low, high)
        new_out[row, ys, :] = jnp.where(full_mask[row, ys, :] == 1, cell, point)
        return carry

    for c in range(chunks):
        lax.fori_loop(c * step * pieces, (c + 1) * step * pieces, last, 0)
        leave(new_out, new_hbm, new_sems, c).start()
    lam_out[0, 0] = lam[0, 0]
    for c in range(chunks):
        leave(obj_out, obj_hbm, obj_sems, c).wait()
        leave(new_out, new_hbm, new_sems, c).wait()

    for one in (r_mask, r_rest, r_a, r_sens, r_vb, *r_ob):
        one.wait_send()
    for two in (r_des, y_v, *y_o):
        sent(two, has_yl, has_yr)
    for two in (x_a, x_v, x_o):
        sent(two, has_xl, has_xr)


def per_device(design, sensitivity, solid_mask):
    rows, ry, depth = design.shape
    half = depth // 2
    nx, ny = lax.axis_size("gx"), lax.axis_size("gy")
    f32 = jnp.float32
    block = (rows, ry, depth)
    wide = (rows, ry + 2 * RADIUS, depth)
    tall = (2 * rows + 2 * RADIUS, ry, half)
    strip = (2 * rows, ry, half)
    anywhere = pl.BlockSpec(memory_space=pl.ANY)
    dma = pltpu.SemaphoreType.DMA
    new_design, objective_grad, lam = pl.pallas_call(
        kernel,
        out_shape=(
            jax.ShapeDtypeStruct(block, f32),
            jax.ShapeDtypeStruct(block, f32),
            jax.ShapeDtypeStruct((1, 1), f32),
        ),
        in_specs=[anywhere] * 3,
        out_specs=(anywhere, anywhere, pl.BlockSpec(memory_space=pltpu.SMEM)),
        scratch_shapes=[
            pltpu.VMEM(block, f32),
            pltpu.VMEM(block, f32),
            pltpu.VMEM(block, f32),
            pltpu.VMEM((8, half), f32),
            pltpu.VMEM(block, jnp.int32),
            pltpu.VMEM(wide, f32),
            pltpu.VMEM(block, f32),
            pltpu.VMEM(tall, f32),
            pltpu.VMEM(strip, jnp.int32),
            pltpu.VMEM(strip, f32),
            pltpu.VMEM(tall, f32),
            pltpu.VMEM(tall, f32),
            pltpu.VMEM(strip, f32),
            pltpu.VMEM(strip, f32),
            pltpu.VMEM(wide, f32),
            pltpu.VMEM(wide, f32),
            pltpu.VMEM((DUAL_ITERS, ny, 8, 128), f32),
            pltpu.VMEM((DUAL_ITERS, nx, 8, 128), f32),
            dma((COUNT,)),
            dma((COUNT,)),
            dma((7,)),
            dma((DUAL_ITERS, ny)),
            dma((DUAL_ITERS, ny)),
            dma((DUAL_ITERS, nx)),
            dma((DUAL_ITERS, nx)),
            dma((CHUNKS,)),
            dma((CHUNKS,)),
        ],
        compiler_params=pltpu.CompilerParams(
            collective_id=0, has_side_effects=True, vmem_limit_bytes=56 * 1024 * 1024
        ),
    )(design, sensitivity, solid_mask)
    return new_design, objective_grad, lam.reshape(())


def solution(mesh):
    return jax.shard_map(
        per_device,
        mesh=mesh,
        in_specs=(P("gx", "gy", None), P("gx", "gy", None), P("gx", "gy", None)),
        out_specs=(P("gx", "gy", None), P("gx", "gy", None), P()),
        check_vma=False,
    )
```
